32 devices in a mesh: row: 16 (over z, x, core), col: 2 (over y).
Axes of the slice: x: 2, y: 2, z: 4, core: 2. Of those that a mesh axis runs over, the one named last changes fastest.
Arguments:
- forcing: float32 [16, 2, 96, 2048], P('row', 'col'), may hold values from -4 to 4
- local_op: bfloat16 [16, 2, 2048, 2048], P('row', 'col'), may hold values from -0.027621359 to 1.0376214
- material: int32 [16, 2, 2048], P('row', 'col'), may hold values from 0 to 7
- stiffness: float32 [8], replicated, may hold values from 0.25 to 4
Outputs:
- preconditioned: float32 [16, 2, 96, 2048], P('row', 'col')
- residual: float32 [16, 2, 96, 2048], P('row', 'col')
The draws below stay inside these ranges and needn't reach their ends.
All inputs are finite; a program needn't handle non-finite values.
Results may differ from the reference program's by a relative error of at most 0.007.
Values may be sent and summed in bfloat16 or wider, within the bound.
A program may use at most 64 MiB of HBM per device.

```python
import math
import jax
import jax.numpy as jnp
from jax import lax

ORDER = 2048
LOADS = 96
CLASSES = 8
N_ROW = 16
N_COL = 2


def draw_local_op(key, part):
    side_width = ORDER // 4
    first_key, second_key = jax.random.split(jax.random.fold_in(key, 11))
    noise = jnp.clip(jax.random.normal(first_key, (N_ROW, N_COL, ORDER, ORDER), jnp.float32), -6.0, 6.0) * (0.2 / math.sqrt(ORDER))
    strength = jax.random.uniform(second_key, (N_ROW, N_COL, ORDER, 1), jnp.float32, math.log(0.3), math.log(30.0))
    carried = jnp.exp(-jnp.exp(strength) / (N_ROW + N_COL))
    incoming = jnp.arange(ORDER, dtype=jnp.int32)[:, None]
    outgoing = jnp.arange(ORDER, dtype=jnp.int32)[None, :]
    side_index = incoming // side_width
    opposite = (side_index + 1 - 2 * (side_index % 2)) * side_width + incoming % side_width
    identity = (incoming == outgoing).astype(jnp.float32)
    crossing = (outgoing == opposite).astype(jnp.float32)
    return (noise + 0.3 * identity + carried * crossing).astype(jnp.bfloat16)


def plant(entries, rng, smallest, largest):
    longest = entries.shape.index(max(entries.shape))
    spots = []
    for shift in (0, 1):
        where = [jax.random.randint(jax.random.fold_in(rng, axis), (), 0, length) for axis, length in enumerate(entries.shape)]
        where[longest] = (where[longest] + shift) % entries.shape[longest]
        spots.append(tuple(where))
    return entries.at[spots[0]].set(smallest).at[spots[1]].set(largest)


def shard_levels(own_key, extent, cuts, least, high):
    factor_of, own = 1.0, jax.random.fold_in(own_key, 6)
    for dim, blocks in cuts:
        draws = jnp.exp(jax.random.uniform(jax.random.fold_in(own, dim), (blocks,), jnp.float32, least / len(cuts), high / len(cuts)))
        factor_of = factor_of * jnp.repeat(draws, extent[dim] // blocks).reshape([-1 if axis == dim else 1 for axis in range(len(extent))])
    return factor_of


def bell_draw(key, dims, width, most, pieces=(), kind=jnp.bfloat16):
    level = shard_levels(key, dims, pieces, -0.22, 0.18) if pieces else 1.0
    entries = jax.random.normal(key, dims, jnp.float32) * width * level
    return jnp.minimum(jnp.maximum(entries, -most), most).astype(kind)


def setup_inputs(seed: int = 0) -> dict:
    seeds = jax.random.split(jax.random.key(seed), 5)
    forcing = bell_draw(seeds[0], (N_ROW, N_COL, LOADS, ORDER), 0.5, 4.0, ((0, 16), (1, 2)), jnp.float32)
    local_op = draw_local_op(jax.random.fold_in(seeds[4], 71), 0)
    material = plant(jax.random.randint(seeds[2], (N_ROW, N_COL, ORDER), 0, CLASSES), jax.random.fold_in(seeds[2], 1), 0, CLASSES - 1).astype(jnp.int32)
    stiffness = jnp.clip(jnp.exp(jax.random.uniform(seeds[3], (CLASSES,), jnp.float32, math.log(0.25), math.log(4.0))), 0.25, 4.0)
    return dict(forcing=forcing, local_op=local_op, material=material, stiffness=stiffness)


def side_block(values, side_index):
    side_width = values.shape[-1] // 4
    return values[..., side_index * side_width:(side_index + 1) * side_width]


def sweep_grid(forcing, local_op, forward_rows, forward_cols):
    side_width = ORDER // 4
    in_row, out_row = (0, 1) if forward_rows else (1, 0)
    in_col, out_col = (2, 3) if forward_cols else (3, 2)

    def cell_step(col_trace, inputs):
        source, matrix, row_trace = inputs
        solved = jnp.dot(source.astype(jnp.bfloat16), matrix, preferred_element_type=jnp.float32)
        solved = solved + jnp.dot(row_trace, matrix[in_row * side_width:(in_row + 1) * side_width], preferred_element_type=jnp.float32)
        solved = solved + jnp.dot(col_trace, matrix[in_col * side_width:(in_col + 1) * side_width], preferred_element_type=jnp.float32)
        next_col = side_block(solved, out_col).astype(jnp.bfloat16)
        next_row = side_block(solved, out_row).astype(jnp.bfloat16)
        return next_col, (solved, next_row)

    def row_step(row_traces, inputs):
        source_row, matrix_row = inputs
        starting = jnp.zeros((LOADS, side_width), jnp.bfloat16)
        unused, (solved_row, next_traces) = lax.scan(cell_step, starting, (source_row, matrix_row, row_traces), reverse=not forward_cols)
        return next_traces, solved_row

    initial = jnp.zeros((N_COL, LOADS, side_width), jnp.bfloat16)
    unused, solved = lax.scan(row_step, initial, (forcing, local_op), reverse=not forward_rows)
    return solved


def reference(forcing, local_op, material, stiffness):
    summed = jnp.zeros(forcing.shape, jnp.float32)
    for forward_rows in (True, False):
        for forward_cols in (True, False):
            summed = summed + sweep_grid(forcing, local_op, forward_rows, forward_cols)
    preconditioned = summed * 0.25
    rounded = lax.optimization_barrier(preconditioned.astype(jnp.bfloat16)).astype(jnp.float32)
    zero_row = jnp.zeros_like(side_block(rounded, 0)[:1])
    zero_col = jnp.zeros_like(side_block(rounded, 0)[:, :1])
    from_above = jnp.concatenate([zero_row, side_block(rounded, 1)[:-1]], axis=0)
    from_below = jnp.concatenate([side_block(rounded, 0)[1:], zero_row], axis=0)
    from_left = jnp.concatenate([zero_col, side_block(rounded, 3)[:, :-1]], axis=1)
    from_right = jnp.concatenate([side_block(rounded, 2)[:, 1:], zero_col], axis=1)
    facing = jnp.concatenate([from_above, from_below, from_left, from_right], axis=-1)
    classes = jnp.arange(CLASSES, dtype=jnp.int32)
    coupling = jnp.sum(jnp.where(material[..., None] == classes, stiffness, 0.0), axis=-1)
    residual = forcing - preconditioned + coupling[:, :, None, :] * (facing - preconditioned)
    return preconditioned, residual
```

```python
import functools

import jax
import jax.numpy as jnp
from jax import lax
from jax.experimental import pallas as pl
from jax.experimental.pallas import tpu as pltpu
from jax.sharding import PartitionSpec as P

MESH = pl.DeviceIdType.MESH


def kernel(
    row_count, col_count, forcing, op, material, stiffness, pre_out, res_out,
    source, half, mat, base, acc, tmp_row, tmp_col, sent, got, rim_sent, rim_got,
    pre, res, classes, load_sem, op_sem, out_sem, sent_sem, got_sem, rim_send_sem, rim_got_sem,
):
    width = base.shape[-1]
    row = lax.axis_index("row")
    col = lax.axis_index("col")

    def columns(side):
        return pl.ds(pl.multiple_of(side * width, width), width)

    low_half = row * 2 < row_count
    order = [jnp.where(low_half, 1, 0), 3, 2, jnp.where(low_half, 0, 1)]
    load_forcing = pltpu.make_async_copy(forcing.at[0, 0], source, load_sem.at[0])
    load_classes = pltpu.make_async_copy(material.at[0], classes, load_sem.at[1])

    def load_op(side):
        return pltpu.make_async_copy(op.at[0, 0, :, columns(side)], mat.at[side], op_sem.at[side])

    load_forcing.start()
    for side in order:
        load_op(side).start()
    load_classes.start()

    below, above = row > 0, row < row_count - 1
    left, right = col > 0, col < col_count - 1
    neighbours = (
        (below, {"row": row - 1}), (above, {"row": row + 1}),
        (left, {"col": col - 1}), (right, {"col": col + 1}),
    )
    barrier = pltpu.get_barrier_semaphore()
    for there, who in neighbours:
        @pl.when(there)
        def _(who=who):
            pl.semaphore_signal(barrier, inc=1, device_id=who, device_id_type=MESH)

    load_forcing.wait()
    half[...] = source[...].astype(jnp.bfloat16)
    acc[...] = jnp.zeros_like(acc)

    for position, side in enumerate(order):
        load_op(side).wait()
        base[side] = jnp.dot(half[...], mat[side], preferred_element_type=jnp.float32)

    count = sum(jnp.where(there, 1, 0) for there, _ in neighbours)
    pl.semaphore_wait(barrier, count)

    ticks = []
    for heading in range(4):
        row_part = row if heading < 2 else row_count - 1 - row
        col_part = col if heading % 2 == 0 else col_count - 1 - col
        ticks.append((row_part + col_part) * 4 + heading)
    ranks = [
        sum(jnp.where(ticks[other] < ticks[mine], 1, 0) for other in range(4) if other != mine)
        for mine in range(4)
    ]

    def trace_copy(heading, kind, who):
        return pltpu.make_async_remote_copy(
            src_ref=sent.at[heading, kind],
            dst_ref=got.at[heading, kind],
            send_sem=sent_sem.at[heading, kind],
            recv_sem=got_sem.at[heading, kind],
            device_id=who,
            device_id_type=MESH,
        )

    def facts(heading):
        back_row, back_col = heading // 2, heading % 2
        to_row, to_col = 1 - 2 * back_row, 1 - 2 * back_col
        next_row, next_col = row + to_row, col + to_col
        last_row, last_col = row - to_row, col - to_col
        has_row = jnp.logical_and(last_row >= 0, last_row < row_count)
        has_col = jnp.logical_and(last_col >= 0, last_col < col_count)
        gives_row = jnp.logical_and(next_row >= 0, next_row < row_count)
        gives_col = jnp.logical_and(next_col >= 0, next_col < col_count)
        return back_row, back_col, next_row, next_col, has_row, has_col, gives_row, gives_col

    def solve(position, carry):
        heading = sum(jnp.where(ranks[h] == position, h, 0) for h in range(4))
        back_row, back_col, next_row, next_col, has_row, has_col, gives_row, gives_col = facts(heading)
        in_row, out_row, in_col, out_col = back_row, 1 - back_row, 2 + back_col, 3 - back_col

        def times(kind, in_side, out_side):
            return jnp.dot(
                got[heading, kind], mat[out_side, columns(in_side), :],
                preferred_element_type=jnp.float32,
            )

        tmp_row[...] = base[out_row]
        tmp_col[...] = base[out_col]

        @pl.when(has_col)
        def _():
            trace_copy(heading, 1, {"col": col}).wait_recv()
            tmp_row[...] += times(1, in_col, out_row)
            tmp_col[...] += times(1, in_col, out_col)

        @pl.when(has_row)
        def _():
            trace_copy(heading, 0, {"row": row}).wait_recv()
            tmp_row[...] += times(0, in_row, out_row)

        @pl.when(gives_row)
        def _():
            sent[heading, 0] = tmp_row[...].astype(jnp.bfloat16)
            trace_copy(heading, 0, {"row": next_row}).start()

        @pl.when(has_row)
        def _():
            tmp_col[...] += times(0, in_row, out_col)

        @pl.when(gives_col)
        def _():
            sent[heading, 1] = tmp_col[...].astype(jnp.bfloat16)
            trace_copy(heading, 1, {"col": next_col}).start()

        acc[out_row] += tmp_row[...]
        acc[out_col] += tmp_col[...]
        acc[in_row] += base[in_row]
        acc[in_col] += base[in_col]

        @pl.when(has_row)
        def _():
            acc[in_row] += times(0, in_row, in_row)
            acc[in_col] += times(0, in_row, in_col)

        @pl.when(has_col)
        def _():
            acc[in_row] += times(1, in_col, in_row)
            acc[in_col] += times(1, in_col, in_col)

        return carry

    lax.fori_loop(0, 4, solve, 0)

    def rim_copy(side, who):
        return pltpu.make_async_remote_copy(
            src_ref=rim_sent.at[side],
            dst_ref=rim_got.at[side ^ 1],
            send_sem=rim_send_sem.at[side],
            recv_sem=rim_got_sem.at[side ^ 1],
            device_id=who,
            device_id_type=MESH,
        )

    def out_copy(kind, side):
        where = pl.ds(side * width, width)
        from_ref, to_ref = ((pre, pre_out), (res, res_out))[kind]
        return pltpu.make_async_copy(
            from_ref.at[side], to_ref.at[0, 0, :, where], out_sem.at[kind, side]
        )

    for side in range(4):
        there, who = neighbours[side]
        value = acc[side] * 0.25
        pre[side] = value
        rim_sent[side] = value.astype(jnp.bfloat16)

        @pl.when(there)
        def _():
            rim_copy(side, who).start()

        @pl.when(jnp.logical_not(there))
        def _():
            rim_got[side] = jnp.zeros_like(rim_got[side])

        out_copy(0, side).start()

    load_classes.wait()
    for side in (0, 1, 2, 3):
        there, who = neighbours[side]
        where = slice(side * width, (side + 1) * width)
        coupling = jnp.zeros((1, width), jnp.float32)
        for index in range(stiffness.shape[0]):
            coupling = coupling + jnp.where(classes[:, where] == index, stiffness[index], 0.0)

        @pl.when(there)
        def _():
            rim_copy(side ^ 1, who).wait_recv()

        value = pre[side]
        facing = rim_got[side].astype(jnp.float32)
        res[side] = source[:, where] - value + coupling * (facing - value)
        out_copy(1, side).start()

    for side in range(4):
        there, who = neighbours[side]

        @pl.when(there)
        def _():
            rim_copy(side, who).wait_send()

        out_copy(0, side).wait()
        out_copy(1, side).wait()
    for heading in range(4):
        _, _, next_row, next_col, _, _, gives_row, gives_col = facts(heading)

        @pl.when(gives_row)
        def _():
            trace_copy(heading, 0, {"row": next_row}).wait_send()

        @pl.when(gives_col)
        def _():
            trace_copy(heading, 1, {"col": next_col}).wait_send()


def local(forcing, local_op, material, stiffness, *, row_count, col_count):
    _, _, loads, order = forcing.shape
    width = order // 4
    side_half = (loads, width)
    any_spec = pl.BlockSpec(memory_space=pl.ANY)
    out = jax.ShapeDtypeStruct(forcing.shape, jnp.float32)
    dma = pltpu.SemaphoreType.DMA
    return pl.pallas_call(
        functools.partial(kernel, row_count, col_count),
        out_shape=(out, out),
        in_specs=[any_spec, any_spec, any_spec, pl.BlockSpec(memory_space=pltpu.SMEM)],
        out_specs=(any_spec, any_spec),
        scratch_shapes=[
            pltpu.VMEM((loads, order), jnp.float32),
            pltpu.VMEM((loads, order), jnp.bfloat16),
            pltpu.VMEM((4, order, width), jnp.bfloat16),
            pltpu.VMEM((4,) + side_half, jnp.float32),
            pltpu.VMEM((4,) + side_half, jnp.float32),
            pltpu.VMEM(side_half, jnp.float32),
            pltpu.VMEM(side_half, jnp.float32),
            pltpu.VMEM((4, 2) + side_half, jnp.bfloat16),
            pltpu.VMEM((4, 2) + side_half, jnp.bfloat16),
            pltpu.VMEM((4,) + side_half, jnp.bfloat16),
            pltpu.VMEM((4,) + side_half, jnp.bfloat16),
            pltpu.VMEM((4,) + side_half, jnp.float32),
            pltpu.VMEM((4,) + side_half, jnp.float32),
            pltpu.VMEM((1, order), jnp.int32),
            dma((2,)),
            dma((4,)),
            dma((2, 4)),
            dma((4, 2)),
            dma((4, 2)),
            dma((4,)),
            dma((4,)),
        ],
        compiler_params=pltpu.CompilerParams(collective_id=0, has_side_effects=True),
    )(forcing, local_op, material, stiffness)


def solution(mesh):
    sizes = dict(mesh.shape)
    return jax.shard_map(
        functools.partial(local, row_count=sizes["row"], col_count=sizes["col"]),
        mesh=mesh,
        in_specs=(
            P("row", "col", None, None),
            P("row", "col", None, None),
            P("row", "col", None),
            P(),
        ),
        out_specs=(P("row", "col", None, None), P("row", "col", None, None)),
        check_vma=False,
    )
```

```python
import functools

import jax
import jax.numpy as jnp
from jax import lax
from jax.experimental import pallas as pl
from jax.experimental.pallas import tpu as pltpu
from jax.sharding import PartitionSpec as P

MESH = pl.DeviceIdType.MESH


def kernel(
    row_count, col_count, forcing, op, material, stiffness, sum_out, facing_out, coupling_out,
    source, half, mat, base, acc, tmp_row, tmp_col, twin_mat, twin_base, cross,
    row_sent, row_got, col_sent, col_got, twin_row, twin_col, rim_sent, rim_got, coupling, classes,
    load_sem, op_sem, out_sem, mat_sem, base_sem, row_sem, col_sem, cross_sem, relay_sem, rim_sem,
):
    width = base.shape[-1]
    row = lax.axis_index("row")
    col = lax.axis_index("col")
    core = row % 2
    pair = row // 2
    pair_count = row_count // 2
    step = 1 - 2 * core
    twin = row + step
    in_row, out_row = core, 1 - core
    left, right = col > 0, col < col_count - 1
    has_row = jnp.where(core == 0, pair, pair_count - 1 - pair) > 0
    gives_row = jnp.where(core == 0, pair_count - 1 - pair, pair) > 0

    def columns(side):
        return pl.ds(pl.multiple_of(side * width, width), width)

    def remote(src, dst, sem, place, who):
        return pltpu.make_async_remote_copy(
            src_ref=src, dst_ref=dst, send_sem=sem.at[(0,) + place], recv_sem=sem.at[(1,) + place],
            device_id=who, device_id_type=MESH,
        )

    def dot(left_value, right_value):
        return jnp.dot(left_value, right_value, preferred_element_type=jnp.float32)

    first = jnp.where(col <= col_count - 1 - col, 0, 1)
    low_half = pair * 2 < pair_count
    order = [jnp.where(low_half, 1, 0), 3 - first, 2 + first, jnp.where(low_half, 0, 1)]
    load_forcing = pltpu.make_async_copy(forcing.at[0, 0], source, load_sem.at[0])
    load_classes = pltpu.make_async_copy(material.at[0], classes, load_sem.at[1])

    def load_op(side):
        return pltpu.make_async_copy(op.at[0, 0, :, columns(side)], mat.at[side], op_sem.at[side])

    load_forcing.start()
    for side in order:
        load_op(side).start()
    load_classes.start()

    partners = (
        (row > 0, {"row": row - 1}), (row < row_count - 1, {"row": row + 1}),
        (row > 1, {"row": row - 2}), (row < row_count - 2, {"row": row + 2}),
        (left, {"col": col - 1}), (right, {"col": col + 1}),
    )
    neighbours = (partners[0], partners[1], partners[4], partners[5])
    barrier = pltpu.get_barrier_semaphore()
    for there, who in partners:
        @pl.when(there)
        def _(who=who):
            pl.semaphore_signal(barrier, inc=1, device_id=who, device_id_type=MESH)
    pl.semaphore_wait(barrier, sum(jnp.where(there, 1, 0) for there, _ in partners))

    def has_col(d):
        return jnp.where(d == 0, col, col_count - 1 - col) > 0

    def gives_col(d):
        return jnp.where(d == 0, col_count - 1 - col, col) > 0

    def mat_copy(slot, in_side, out_side):
        return remote(
            op.at[0, 0, columns(in_side), columns(out_side)], twin_mat.at[slot], mat_sem, (slot,),
            {"row": twin},
        )

    twin_in, twin_out = 1 - core, core
    shared = [(row >= 0, 0, twin_in, twin_out)]
    for d in (0, 1):
        enters, leaves = has_col(d), gives_col(d)
        shared.append((leaves, 1 + 3 * d, twin_in, 3 - d))
        shared.append((enters, 2 + 3 * d, 2 + d, twin_out))
        shared.append((jnp.logical_and(enters, leaves), 3 + 3 * d, 2 + d, 3 - d))

    def all_shared(act):
        for there, slot, in_side, out_side in shared:
            @pl.when(there)
            def _(slot=slot, in_side=in_side, out_side=out_side):
                act(mat_copy(slot, in_side, out_side))

    all_shared(lambda copy: copy.start())

    def base_copy(slot, side):
        return remote(base.at[side], twin_base.at[slot], base_sem, (slot,), {"row": twin})

    load_forcing.wait()
    half[...] = source[...].astype(jnp.bfloat16)

    def make_base(side):
        load_op(side).wait()
        base[side] = dot(half[...], mat[side])

        @pl.when(side == twin_out)
        def _():
            base_copy(0, side).start()

        for d in (0, 1):
            @pl.when(jnp.logical_and(side == 3 - d, gives_col(d)))
            def _(d=d):
                base_copy(1 + d, side).start()

    def row_copy(d):
        return remote(
            row_sent.at[d], row_got.at[d], row_sem, (d,), {"row": row + 2 * step}
        )

    def col_copy(d, cell):
        return remote(
            col_sent.at[d, cell], col_got.at[d, cell], col_sem, (d, cell), {"col": col + 1 - 2 * d}
        )

    def cross_copy(d):
        return remote(cross.at[d], twin_row.at[d], cross_sem, (d,), {"row": twin})

    def relay_copy(d):
        return remote(col_got.at[d, 1], twin_col.at[d], relay_sem, (d,), {"row": twin})

    def solve(d, wait_shared):
        in_col, out_col = 2 + d, 3 - d
        enters, leaves = has_col(d), gives_col(d)
        tmp_row[0] = base[out_row]

        if wait_shared:
            base_copy(0, out_row).wait_recv()
            mat_copy(0, twin_in, twin_out).wait_recv()
        tmp_row[1] = twin_base[0]

        @pl.when(enters)
        def _():
            col_copy(d, 0).wait_recv()
            tmp_row[0] += dot(col_got[d, 0], mat[out_row, columns(in_col), :])
            mat_copy(2 + 3 * d, 0, 0).wait_recv()
            col_copy(d, 1).wait_recv()
            relay_copy(d).start()
            tmp_row[1] += dot(col_got[d, 1], twin_mat[2 + 3 * d])

        @pl.when(has_row)
        def _():
            row_copy(d).wait_recv()
            tmp_row[0] += dot(row_got[d], mat[out_row, columns(in_row), :])

        cross[d] = tmp_row[0].astype(jnp.bfloat16)

        @pl.when(gives_row)
        def _():
            row_sent[d] = (tmp_row[1] + dot(cross[d], twin_mat[0])).astype(jnp.bfloat16)
            row_copy(d).start()

        @pl.when(leaves)
        def _():
            tmp_col[...] = base[out_col]

            @pl.when(enters)
            def _():
                tmp_col[...] += dot(col_got[d, 0], mat[out_col, columns(in_col), :])

            @pl.when(has_row)
            def _():
                tmp_col[...] += dot(row_got[d], mat[out_col, columns(in_row), :])

            col_sent[d, 0] = tmp_col[...].astype(jnp.bfloat16)
            col_copy(d, 0).start()
            base_copy(1 + d, 0).wait_recv()
            mat_copy(1 + 3 * d, 0, 0).wait_recv()
            tmp_col[...] = twin_base[1 + d] + dot(cross[d], twin_mat[1 + 3 * d])

            @pl.when(enters)
            def _():
                mat_copy(3 + 3 * d, 0, 0).wait_recv()
                tmp_col[...] += dot(col_got[d, 1], twin_mat[3 + 3 * d])

            col_sent[d, 1] = tmp_col[...].astype(jnp.bfloat16)
            col_copy(d, 1).start()

        cross_copy(d).start()

    def add_terms(trace, in_side):
        def one(side, carry):
            acc[side] += dot(trace[...], mat[side, columns(in_side), :])
            return carry

        lax.fori_loop(0, 4, one, 0)

    def own_terms(d):
        @pl.when(has_row)
        def _():
            add_terms(row_got.at[d], in_row)

        @pl.when(has_col(d))
        def _():
            add_terms(col_got.at[d, 0], 2 + d)

    def twin_terms():
        def one(position, carry):
            d = jnp.where(position == 0, first, 1 - first)
            cross_copy(d).wait_recv()
            add_terms(twin_row.at[d], 1 - core)

            @pl.when(has_col(d))
            def _():
                relay_copy(d).wait_recv()
                add_terms(twin_col.at[d], 2 + d)

            return carry

        lax.fori_loop(0, 2, one, 0)

    make_base(order[0])
    make_base(order[1])
    early = jnp.logical_and(
        jnp.where(low_half, 0, 1) == core,
        jnp.logical_not(jnp.logical_or(has_row, has_col(first))),
    )

    @pl.when(early)
    def _():
        solve(first, True)

    make_base(order[2])
    make_base(order[3])
    acc[...] = base[...] * 4.0

    depth = jnp.where(core == 0, pair, pair_count - 1 - pair)
    twin_first = depth * 2 >= pair_count + 2

    @pl.when(twin_first)
    def _():
        twin_terms()

    @pl.when(jnp.logical_not(early))
    def _():
        solve(first, True)

    own_terms(first)
    solve(1 - first, False)
    own_terms(1 - first)

    @pl.when(jnp.logical_not(twin_first))
    def _():
        twin_terms()

    def rim_copy(side, who):
        return pltpu.make_async_remote_copy(
            src_ref=rim_sent.at[side], dst_ref=rim_got.at[side ^ 1],
            send_sem=rim_sem.at[0, side], recv_sem=rim_sem.at[1, side ^ 1],
            device_id=who, device_id_type=MESH,
        )

    def out_copy(kind, side):
        where = pl.ds(side * width, width)
        from_ref, to_ref = ((acc, sum_out), (rim_got, facing_out))[kind]
        return pltpu.make_async_copy(
            from_ref.at[side], to_ref.at[0, 0, :, where], out_sem.at[kind, side]
        )

    for side in range(4):
        there, who = neighbours[side]
        rim_sent[side] = (acc[side] * 0.25).astype(jnp.bfloat16)

        @pl.when(there)
        def _():
            rim_copy(side, who).start()

        @pl.when(jnp.logical_not(there))
        def _():
            rim_got[side] = jnp.zeros_like(rim_got[side])

        out_copy(0, side).start()

    load_classes.wait()
    total = jnp.zeros(coupling.shape, jnp.float32)
    for index in range(stiffness.shape[0]):
        total = total + jnp.where(classes[...] == index, stiffness[index], 0.0)
    coupling[...] = total
    coupling_copy = pltpu.make_async_copy(coupling, coupling_out.at[0], load_sem.at[2])
    coupling_copy.start()

    for side in range(4):
        there, who = neighbours[side]

        @pl.when(there)
        def _():
            rim_copy(side ^ 1, who).wait_recv()

        out_copy(1, side).start()

    for side in range(4):
        there, who = neighbours[side]

        @pl.when(there)
        def _():
            rim_copy(side, who).wait_send()

        out_copy(0, side).wait()
        out_copy(1, side).wait()
    coupling_copy.wait()
    all_shared(lambda copy: copy.wait_send())
    base_copy(0, 0).wait_send()
    for d in (0, 1):
        cross_copy(d).wait_send()

        @pl.when(gives_row)
        def _():
            row_copy(d).wait_send()

        @pl.when(has_col(d))
        def _():
            relay_copy(d).wait_send()

        @pl.when(gives_col(d))
        def _():
            base_copy(1 + d, 0).wait_send()
            col_copy(d, 0).wait_send()
            col_copy(d, 1).wait_send()


def local(forcing, local_op, material, stiffness, *, row_count, col_count):
    _, _, loads, order = forcing.shape
    width = order // 4
    side = (loads, width)
    any_spec = pl.BlockSpec(memory_space=pl.ANY)
    dma = pltpu.SemaphoreType.DMA
    f32, b16 = jnp.float32, jnp.bfloat16
    summed, facing, coupling = pl.pallas_call(
        functools.partial(kernel, row_count, col_count),
        out_shape=(
            jax.ShapeDtypeStruct(forcing.shape, f32),
            jax.ShapeDtypeStruct(forcing.shape, b16),
            jax.ShapeDtypeStruct(material.shape, f32),
        ),
        in_specs=[any_spec, any_spec, any_spec, pl.BlockSpec(memory_space=pltpu.SMEM)],
        out_specs=(any_spec,) * 3,
        scratch_shapes=[
            pltpu.VMEM((loads, order), f32),
            pltpu.VMEM((loads, order), b16),
            pltpu.VMEM((4, order, width), b16),
            pltpu.VMEM((4,) + side, f32),
            pltpu.VMEM((4,) + side, f32),
            pltpu.VMEM((2,) + side, f32),
            pltpu.VMEM(side, f32),
            pltpu.VMEM((7, width, width), b16),
            pltpu.VMEM((3,) + side, f32),
            pltpu.VMEM((2,) + side, b16),
            pltpu.VMEM((2,) + side, b16),
            pltpu.VMEM((2,) + side, b16),
            pltpu.VMEM((2, 2) + side, b16),
            pltpu.VMEM((2, 2) + side, b16),
            pltpu.VMEM((2,) + side, b16),
            pltpu.VMEM((2,) + side, b16),
            pltpu.VMEM((4,) + side, b16),
            pltpu.VMEM((4,) + side, b16),
            pltpu.VMEM((1, order), f32),
            pltpu.VMEM((1, order), jnp.int32),
            dma((3,)),
            dma((4,)),
            dma((2, 4)),
            dma((2, 7)),
            dma((2, 3)),
            dma((2, 2)),
            dma((2, 2, 2)),
            dma((2, 2)),
            dma((2, 2)),
            dma((2, 4)),
        ],
        compiler_params=pltpu.CompilerParams(collective_id=0, has_side_effects=True),
    )(forcing, local_op, material, stiffness)
    preconditioned = summed * 0.25
    gap = facing.astype(f32) - preconditioned
    residual = forcing - preconditioned + coupling[:, :, None, :] * gap
    return preconditioned, residual


def solution(mesh):
    sizes = dict(mesh.shape)
    return jax.shard_map(
        functools.partial(local, row_count=sizes["row"], col_count=sizes["col"]),
        mesh=mesh,
        in_specs=(
            P("row", "col", None, None),
            P("row", "col", None, None),
            P("row", "col", None),
            P(),
        ),
        out_specs=(P("row", "col", None, None), P("row", "col", None, None)),
        check_vma=False,
    )
```

```python
import functools

import jax
import jax.numpy as jnp
from jax import lax
from jax.experimental import pallas as pl
from jax.experimental.pallas import tpu as pltpu
from jax.sharding import PartitionSpec as P

MESH = pl.DeviceIdType.MESH


def kernel(
    row_count, col_count, forcing, op, material, stiffness, sum_out, facing_out, coupling_out,
    source, half, mat, base, acc, tmp_row, tmp_col, twin_mat, twin_base, cross,
    row_sent, row_got, col_sent, col_got, twin_row, twin_col, rim_sent, rim_got, coupling, classes,
    load_sem, op_sem, out_sem, mat_sem, base_sem, row_sem, col_sem, cross_sem, relay_sem, rim_sem,
):
    width = base.shape[-1]
    chunks = row_sem.shape[-1]
    span = base.shape[1] // chunks
    row = lax.axis_index("row")
    col = lax.axis_index("col")
    core = row % 2
    pair = row // 2
    pair_count = row_count // 2
    step = 1 - 2 * core
    twin = row + step
    in_row, out_row = core, 1 - core
    left, right = col > 0, col < col_count - 1
    has_row = jnp.where(core == 0, pair, pair_count - 1 - pair) > 0
    gives_row = jnp.where(core == 0, pair_count - 1 - pair, pair) > 0

    def columns(side):
        return pl.ds(pl.multiple_of(side * width, width), width)

    def remote(src, dst, sem, place, who):
        return pltpu.make_async_remote_copy(
            src_ref=src, dst_ref=dst, send_sem=sem.at[(0,) + place], recv_sem=sem.at[(1,) + place],
            device_id=who, device_id_type=MESH,
        )

    def dot(left_value, right_value):
        return jnp.dot(left_value, right_value, preferred_element_type=jnp.float32)

    first = jnp.where(col <= col_count - 1 - col, 0, 1)
    low_half = pair * 2 < pair_count
    order = [jnp.where(low_half, 1, 0), 3 - first, 2 + first, jnp.where(low_half, 0, 1)]
    load_forcing = pltpu.make_async_copy(forcing.at[0, 0], source, load_sem.at[0])
    load_classes = pltpu.make_async_copy(material.at[0], classes, load_sem.at[1])

    def load_op(side):
        return pltpu.make_async_copy(op.at[0, 0, :, columns(side)], mat.at[side], op_sem.at[side])

    load_forcing.start()
    for side in order:
        load_op(side).start()
    load_classes.start()

    partners = (
        (row > 0, {"row": row - 1}), (row < row_count - 1, {"row": row + 1}),
        (row > 1, {"row": row - 2}), (row < row_count - 2, {"row": row + 2}),
        (left, {"col": col - 1}), (right, {"col": col + 1}),
    )
    neighbours = (partners[0], partners[1], partners[4], partners[5])
    barrier = pltpu.get_barrier_semaphore()
    for there, who in partners:
        @pl.when(there)
        def _(who=who):
            pl.semaphore_signal(barrier, inc=1, device_id=who, device_id_type=MESH)
    pl.semaphore_wait(barrier, sum(jnp.where(there, 1, 0) for there, _ in partners))

    def has_col(d):
        return jnp.where(d == 0, col, col_count - 1 - col) > 0

    def gives_col(d):
        return jnp.where(d == 0, col_count - 1 - col, col) > 0

    def mat_copy(slot, in_side, out_side):
        return remote(
            op.at[0, 0, columns(in_side), columns(out_side)], twin_mat.at[slot], mat_sem, (slot,),
            {"row": twin},
        )

    twin_in, twin_out = 1 - core, core
    shared = [(row >= 0, 0, twin_in, twin_out)]
    for d in (0, 1):
        enters, leaves = has_col(d), gives_col(d)
        shared.append((leaves, 1 + 3 * d, twin_in, 3 - d))
        shared.append((enters, 2 + 3 * d, 2 + d, twin_out))
        shared.append((jnp.logical_and(enters, leaves), 3 + 3 * d, 2 + d, 3 - d))

    def all_shared(act):
        for there, slot, in_side, out_side in shared:
            @pl.when(there)
            def _(slot=slot, in_side=in_side, out_side=out_side):
                act(mat_copy(slot, in_side, out_side))

    all_shared(lambda copy: copy.start())

    def base_copy(slot, side):
        return remote(base.at[side], twin_base.at[slot], base_sem, (slot,), {"row": twin})

    load_forcing.wait()
    half[...] = source[...].astype(jnp.bfloat16)

    def make_base(side):
        load_op(side).wait()
        base[side] = dot(half[...], mat[side])

        @pl.when(side == twin_out)
        def _():
            base_copy(0, side).start()

        for d in (0, 1):
            @pl.when(jnp.logical_and(side == 3 - d, gives_col(d)))
            def _(d=d):
                base_copy(1 + d, side).start()

    def row_copy(d, chunk):
        part = pl.ds(chunk * span, span)
        return remote(
            row_sent.at[d, part], row_got.at[d, part], row_sem, (d, chunk), {"row": row + 2 * step}
        )

    def col_copy(d, cell):
        return remote(
            col_sent.at[d, cell], col_got.at[d, cell], col_sem, (d, cell), {"col": col + 1 - 2 * d}
        )

    def cross_copy(d):
        return remote(cross.at[d], twin_row.at[d], cross_sem, (d,), {"row": twin})

    def relay_copy(d):
        return remote(col_got.at[d, 1], twin_col.at[d], relay_sem, (d,), {"row": twin})

    def solve(d, wait_shared):
        in_col, out_col = 2 + d, 3 - d
        enters, leaves = has_col(d), gives_col(d)
        tmp_row[0] = base[out_row]

        if wait_shared:
            base_copy(0, out_row).wait_recv()
            mat_copy(0, twin_in, twin_out).wait_recv()
        tmp_row[1] = twin_base[0]

        @pl.when(enters)
        def _():
            col_copy(d, 0).wait_recv()
            tmp_row[0] += dot(col_got[d, 0], mat[out_row, columns(in_col), :])
            mat_copy(2 + 3 * d, 0, 0).wait_recv()
            col_copy(d, 1).wait_recv()
            relay_copy(d).start()
            tmp_row[1] += dot(col_got[d, 1], twin_mat[2 + 3 * d])

        for chunk in range(chunks):
            part = pl.ds(chunk * span, span)

            @pl.when(has_row)
            def _():
                row_copy(d, chunk).wait_recv()
                cross[d, part] = (
                    tmp_row[0, part] + dot(row_got[d, part], mat[out_row, columns(in_row), :])
                ).astype(jnp.bfloat16)

            @pl.when(jnp.logical_not(has_row))
            def _():
                cross[d, part] = tmp_row[0, part].astype(jnp.bfloat16)

            @pl.when(gives_row)
            def _():
                row_sent[d, part] = (
                    tmp_row[1, part] + dot(cross[d, part], twin_mat[0])
                ).astype(jnp.bfloat16)
                row_copy(d, chunk).start()

        cross_copy(d).start()

        @pl.when(leaves)
        def _():
            tmp_col[...] = base[out_col]

            @pl.when(enters)
            def _():
                tmp_col[...] += dot(col_got[d, 0], mat[out_col, columns(in_col), :])

            @pl.when(has_row)
            def _():
                tmp_col[...] += dot(row_got[d], mat[out_col, columns(in_row), :])

            col_sent[d, 0] = tmp_col[...].astype(jnp.bfloat16)
            col_copy(d, 0).start()
            base_copy(1 + d, 0).wait_recv()
            mat_copy(1 + 3 * d, 0, 0).wait_recv()
            tmp_col[...] = twin_base[1 + d] + dot(cross[d], twin_mat[1 + 3 * d])

            @pl.when(enters)
            def _():
                mat_copy(3 + 3 * d, 0, 0).wait_recv()
                tmp_col[...] += dot(col_got[d, 1], twin_mat[3 + 3 * d])

            col_sent[d, 1] = tmp_col[...].astype(jnp.bfloat16)
            col_copy(d, 1).start()

    def add_terms(trace, in_side):
        for side in range(4):
            acc[side] += dot(trace[...], mat[side, columns(in_side), :])

    def own_terms(d):
        @pl.when(has_row)
        def _():
            add_terms(row_got.at[d], in_row)

        @pl.when(has_col(d))
        def _():
            add_terms(col_got.at[d, 0], 2 + d)

    def twin_terms():
        def one(position, carry):
            d = jnp.where(position == 0, first, 1 - first)
            cross_copy(d).wait_recv()
            add_terms(twin_row.at[d], 1 - core)

            @pl.when(has_col(d))
            def _():
                relay_copy(d).wait_recv()
                add_terms(twin_col.at[d], 2 + d)

            return carry

        lax.fori_loop(0, 2, one, 0)

    make_base(order[0])
    make_base(order[1])
    early = jnp.logical_and(
        jnp.where(low_half, 0, 1) == core,
        jnp.logical_not(jnp.logical_or(has_row, has_col(first))),
    )

    @pl.when(early)
    def _():
        solve(first, True)

    make_base(order[2])
    make_base(order[3])
    acc[...] = base[...] * 4.0

    depth = jnp.where(core == 0, pair, pair_count - 1 - pair)
    twin_first = depth * 2 >= pair_count + 2

    @pl.when(twin_first)
    def _():
        twin_terms()

    @pl.when(jnp.logical_not(early))
    def _():
        solve(first, True)

    own_terms(first)
    solve(1 - first, False)
    own_terms(1 - first)

    @pl.when(jnp.logical_not(twin_first))
    def _():
        twin_terms()

    def rim_copy(side, who):
        return pltpu.make_async_remote_copy(
            src_ref=rim_sent.at[side], dst_ref=rim_got.at[side ^ 1],
            send_sem=rim_sem.at[0, side], recv_sem=rim_sem.at[1, side ^ 1],
            device_id=who, device_id_type=MESH,
        )

    def out_copy(kind, side):
        where = pl.ds(side * width, width)
        from_ref, to_ref = ((acc, sum_out), (rim_got, facing_out))[kind]
        return pltpu.make_async_copy(
            from_ref.at[side], to_ref.at[0, 0, :, where], out_sem.at[kind, side]
        )

    for side in range(4):
        there, who = neighbours[side]
        rim_sent[side] = (acc[side] * 0.25).astype(jnp.bfloat16)

        @pl.when(there)
        def _():
            rim_copy(side, who).start()

        @pl.when(jnp.logical_not(there))
        def _():
            rim_got[side] = jnp.zeros_like(rim_got[side])

        out_copy(0, side).start()

    load_classes.wait()
    total = jnp.zeros(coupling.shape, jnp.float32)
    for index in range(stiffness.shape[0]):
        total = total + jnp.where(classes[...] == index, stiffness[index], 0.0)
    coupling[...] = total
    coupling_copy = pltpu.make_async_copy(coupling, coupling_out.at[0], load_sem.at[2])
    coupling_copy.start()

    for side in range(4):
        there, who = neighbours[side]

        @pl.when(there)
        def _():
            rim_copy(side ^ 1, who).wait_recv()

        out_copy(1, side).start()

    for side in range(4):
        there, who = neighbours[side]

        @pl.when(there)
        def _():
            rim_copy(side, who).wait_send()

        out_copy(0, side).wait()
        out_copy(1, side).wait()
    coupling_copy.wait()
    all_shared(lambda copy: copy.wait_send())
    base_copy(0, 0).wait_send()
    for d in (0, 1):
        cross_copy(d).wait_send()

        @pl.when(gives_row)
        def _():
            for chunk in range(chunks):
                row_copy(d, chunk).wait_send()

        @pl.when(has_col(d))
        def _():
            relay_copy(d).wait_send()

        @pl.when(gives_col(d))
        def _():
            base_copy(1 + d, 0).wait_send()
            col_copy(d, 0).wait_send()
            col_copy(d, 1).wait_send()


def local(forcing, local_op, material, stiffness, *, row_count, col_count):
    _, _, loads, order = forcing.shape
    width = order // 4
    side = (loads, width)
    chunks = 2 if loads % 32 == 0 else 1
    any_spec = pl.BlockSpec(memory_space=pl.ANY)
    dma = pltpu.SemaphoreType.DMA
    f32, b16 = jnp.float32, jnp.bfloat16
    summed, facing, coupling = pl.pallas_call(
        functools.partial(kernel, row_count, col_count),
        out_shape=(
            jax.ShapeDtypeStruct(forcing.shape, f32),
            jax.ShapeDtypeStruct(forcing.shape, b16),
            jax.ShapeDtypeStruct(material.shape, f32),
        ),
        in_specs=[any_spec, any_spec, any_spec, pl.BlockSpec(memory_space=pltpu.SMEM)],
        out_specs=(any_spec,) * 3,
        scratch_shapes=[
            pltpu.VMEM((loads, order), f32),
            pltpu.VMEM((loads, order), b16),
            pltpu.VMEM((4, order, width), b16),
            pltpu.VMEM((4,) + side, f32),
            pltpu.VMEM((4,) + side, f32),
            pltpu.VMEM((2,) + side, f32),
            pltpu.VMEM(side, f32),
            pltpu.VMEM((7, width, width), b16),
            pltpu.VMEM((3,) + side, f32),
            pltpu.VMEM((2,) + side, b16),
            pltpu.VMEM((2,) + side, b16),
            pltpu.VMEM((2,) + side, b16),
            pltpu.VMEM((2, 2) + side, b16),
            pltpu.VMEM((2, 2) + side, b16),
            pltpu.VMEM((2,) + side, b16),
            pltpu.VMEM((2,) + side, b16),
            pltpu.VMEM((4,) + side, b16),
            pltpu.VMEM((4,) + side, b16),
            pltpu.VMEM((1, order), f32),
            pltpu.VMEM((1, order), jnp.int32),
            dma((3,)),
            dma((4,)),
            dma((2, 4)),
            dma((2, 7)),
            dma((2, 3)),
            dma((2, 2, chunks)),
            dma((2, 2, 2)),
            dma((2, 2)),
            dma((2, 2)),
            dma((2, 4)),
        ],
        compiler_params=pltpu.CompilerParams(collective_id=0, has_side_effects=True),
    )(forcing, local_op, material, stiffness)
    preconditioned = summed * 0.25
    gap = facing.astype(f32) - preconditioned
    residual = forcing - preconditioned + coupling[:, :, None, :] * gap
    return preconditioned, residual


def solution(mesh):
    sizes = dict(mesh.shape)
    return jax.shard_map(
        functools.partial(local, row_count=sizes["row"], col_count=sizes["col"]),
        mesh=mesh,
        in_specs=(
            P("row", "col", None, None),
            P("row", "col", None, None),
            P("row", "col", None),
            P(),
        ),
        out_specs=(P("row", "col", None, None), P("row", "col", None, None)),
        check_vma=False,
    )
```

```python
import functools

import jax
import jax.numpy as jnp
from jax import lax
from jax.experimental import pallas as pl
from jax.experimental.pallas import tpu as pltpu
from jax.sharding import PartitionSpec as P

MESH = pl.DeviceIdType.MESH


def kernel(
    row_count, col_count, forcing, op, material, stiffness, sum_out, facing_out, coupling_out,
    source, half, mat, base, acc, tmp_row, tmp_col, twin_mat, twin_base, hop, cross,
    row_sent, row_got, col_sent, col_got, twin_row, twin_col, rim_sent, rim_got, coupling, classes,
    load_sem, op_sem, out_sem, mat_sem, base_sem, row_sem, col_sem, cross_sem, relay_sem, rim_sem,
):
    width = base.shape[-1]
    chunks = row_sem.shape[-1]
    span = base.shape[1] // chunks
    row = lax.axis_index("row")
    col = lax.axis_index("col")
    core = row % 2
    pair = row // 2
    pair_count = row_count // 2
    step = 1 - 2 * core
    twin = row + step
    in_row, out_row = core, 1 - core
    left, right = col > 0, col < col_count - 1
    has_row = jnp.where(core == 0, pair, pair_count - 1 - pair) > 0
    gives_row = jnp.where(core == 0, pair_count - 1 - pair, pair) > 0

    def columns(side):
        return pl.ds(pl.multiple_of(side * width, width), width)

    def remote(src, dst, sem, place, who):
        return pltpu.make_async_remote_copy(
            src_ref=src, dst_ref=dst, send_sem=sem.at[(0,) + place], recv_sem=sem.at[(1,) + place],
            device_id=who, device_id_type=MESH,
        )

    def dot(left_value, right_value):
        return jnp.dot(left_value, right_value, preferred_element_type=jnp.float32)

    first = jnp.where(col <= col_count - 1 - col, 0, 1)
    low_half = pair * 2 < pair_count
    order = [jnp.where(low_half, 1, 0), 3 - first, 2 + first, jnp.where(low_half, 0, 1)]
    load_forcing = pltpu.make_async_copy(forcing.at[0, 0], source, load_sem.at[0])
    load_classes = pltpu.make_async_copy(material.at[0], classes, load_sem.at[1])

    def load_op(side):
        return pltpu.make_async_copy(op.at[0, 0, :, columns(side)], mat.at[side], op_sem.at[side])

    load_forcing.start()
    for side in order:
        load_op(side).start()
    load_classes.start()

    partners = (
        (row > 0, {"row": row - 1}), (row < row_count - 1, {"row": row + 1}),
        (row > 1, {"row": row - 2}), (row < row_count - 2, {"row": row + 2}),
        (left, {"col": col - 1}), (right, {"col": col + 1}),
    )
    neighbours = (partners[0], partners[1], partners[4], partners[5])
    barrier = pltpu.get_barrier_semaphore()
    for there, who in partners:
        @pl.when(there)
        def _(who=who):
            pl.semaphore_signal(barrier, inc=1, device_id=who, device_id_type=MESH)
    pl.semaphore_wait(barrier, sum(jnp.where(there, 1, 0) for there, _ in partners))

    def has_col(d):
        return jnp.where(d == 0, col, col_count - 1 - col) > 0

    def gives_col(d):
        return jnp.where(d == 0, col_count - 1 - col, col) > 0

    def mat_copy(slot, in_side, out_side):
        return remote(
            op.at[0, 0, columns(in_side), columns(out_side)], twin_mat.at[slot], mat_sem, (slot,),
            {"row": twin},
        )

    twin_in, twin_out = 1 - core, core
    shared = [(row >= 0, 0, twin_in, twin_out)]
    for d in (0, 1):
        enters, leaves = has_col(d), gives_col(d)
        shared.append((leaves, 1 + 3 * d, twin_in, 3 - d))
        shared.append((enters, 2 + 3 * d, 2 + d, twin_out))
        shared.append((jnp.logical_and(enters, leaves), 3 + 3 * d, 2 + d, 3 - d))

    def all_shared(act):
        for there, slot, in_side, out_side in shared:
            @pl.when(there)
            def _(slot=slot, in_side=in_side, out_side=out_side):
                act(mat_copy(slot, in_side, out_side))

    all_shared(lambda copy: copy.start())

    def base_copy(slot, side):
        return remote(base.at[side], twin_base.at[slot], base_sem, (slot,), {"row": twin})

    load_forcing.wait()
    half[...] = source[...].astype(jnp.bfloat16)

    def make_base(side):
        load_op(side).wait()
        base[side] = dot(half[...], mat[side])

        @pl.when(side == twin_out)
        def _():
            base_copy(0, side).start()

        for d in (0, 1):
            @pl.when(jnp.logical_and(side == 3 - d, gives_col(d)))
            def _(d=d):
                base_copy(1 + d, side).start()

    def row_copy(d, chunk):
        part = pl.ds(chunk * span, span)
        return remote(
            row_sent.at[d, part], row_got.at[d, part], row_sem, (d, chunk), {"row": row + 2 * step}
        )

    def col_copy(d, cell):
        return remote(
            col_sent.at[d, cell], col_got.at[d, cell], col_sem, (d, cell), {"col": col + 1 - 2 * d}
        )

    def cross_copy(d):
        return remote(cross.at[d], twin_row.at[d], cross_sem, (d,), {"row": twin})

    def relay_copy(d):
        return remote(col_got.at[d, 1], twin_col.at[d], relay_sem, (d,), {"row": twin})

    def wait_shared():
        base_copy(0, 0).wait_recv()
        mat_copy(0, 0, 0).wait_recv()

    def solve_row(d):
        in_col = 2 + d
        enters = has_col(d)
        tmp_row[0] = base[out_row]
        tmp_row[1] = twin_base[0]

        @pl.when(enters)
        def _():
            col_copy(d, 0).wait_recv()
            tmp_row[0] += dot(col_got[d, 0], mat[out_row, columns(in_col), :])

        @pl.when(gives_row)
        def _():
            tmp_row[1] += dot(tmp_row[0].astype(jnp.bfloat16), twin_mat[0])

        @pl.when(enters)
        def _():
            mat_copy(2 + 3 * d, 0, 0).wait_recv()
            col_copy(d, 1).wait_recv()
            relay_copy(d).start()
            tmp_row[1] += dot(col_got[d, 1], twin_mat[2 + 3 * d])

        for chunk in range(chunks):
            part = pl.ds(chunk * span, span)

            @pl.when(has_row)
            def _():
                row_copy(d, chunk).wait_recv()

            @pl.when(jnp.logical_and(has_row, gives_row))
            def _():
                row_sent[d, part] = (
                    tmp_row[1, part] + dot(row_got[d, part], hop[...])
                ).astype(jnp.bfloat16)
                row_copy(d, chunk).start()

            @pl.when(jnp.logical_and(jnp.logical_not(has_row), gives_row))
            def _():
                row_sent[d, part] = tmp_row[1, part].astype(jnp.bfloat16)
                row_copy(d, chunk).start()

        @pl.when(has_row)
        def _():
            tmp_row[0] += dot(row_got[d], mat[out_row, columns(in_row), :])

        cross[d] = tmp_row[0].astype(jnp.bfloat16)
        cross_copy(d).start()

    def solve_col(d):
        in_col, out_col = 2 + d, 3 - d
        enters, leaves = has_col(d), gives_col(d)

        @pl.when(leaves)
        def _():
            tmp_col[...] = base[out_col]

            @pl.when(enters)
            def _():
                tmp_col[...] += dot(col_got[d, 0], mat[out_col, columns(in_col), :])

            @pl.when(has_row)
            def _():
                tmp_col[...] += dot(row_got[d], mat[out_col, columns(in_row), :])

            col_sent[d, 0] = tmp_col[...].astype(jnp.bfloat16)
            col_copy(d, 0).start()
            base_copy(1 + d, 0).wait_recv()
            mat_copy(1 + 3 * d, 0, 0).wait_recv()
            tmp_col[...] = twin_base[1 + d] + dot(cross[d], twin_mat[1 + 3 * d])

            @pl.when(enters)
            def _():
                mat_copy(3 + 3 * d, 0, 0).wait_recv()
                tmp_col[...] += dot(col_got[d, 1], twin_mat[3 + 3 * d])

            col_sent[d, 1] = tmp_col[...].astype(jnp.bfloat16)
            col_copy(d, 1).start()

    def add_terms(trace, in_side):
        for side in range(4):
            acc[side] += dot(trace[...], mat[side, columns(in_side), :])

    def own_terms(d):
        @pl.when(has_row)
        def _():
            add_terms(row_got.at[d], in_row)

        @pl.when(has_col(d))
        def _():
            add_terms(col_got.at[d, 0], 2 + d)

    def twin_terms():
        def one(position, carry):
            d = jnp.where(position == 0, first, 1 - first)
            cross_copy(d).wait_recv()
            add_terms(twin_row.at[d], 1 - core)

            @pl.when(has_col(d))
            def _():
                relay_copy(d).wait_recv()
                add_terms(twin_col.at[d], 2 + d)

            return carry

        lax.fori_loop(0, 2, one, 0)

    early = jnp.logical_and(
        jnp.where(low_half, 0, 1) == core,
        jnp.logical_not(jnp.logical_or(has_row, has_col(first))),
    )
    make_base(order[0])

    @pl.when(early)
    def _():
        wait_shared()
        solve_row(first)

    make_base(order[1])

    @pl.when(early)
    def _():
        solve_col(first)

    make_base(order[2])
    make_base(order[3])
    acc[...] = base[...] * 4.0

    @pl.when(jnp.logical_not(early))
    def _():
        wait_shared()

    @pl.when(jnp.logical_and(has_row, gives_row))
    def _():
        hop[...] = dot(mat[out_row, columns(in_row), :], twin_mat[0]).astype(jnp.bfloat16)

    depth = jnp.where(core == 0, pair, pair_count - 1 - pair)
    twin_first = depth * 2 >= pair_count + 2

    @pl.when(twin_first)
    def _():
        twin_terms()

    @pl.when(jnp.logical_not(early))
    def _():
        solve_row(first)
        solve_col(first)

    own_terms(first)
    solve_row(1 - first)
    solve_col(1 - first)
    own_terms(1 - first)

    @pl.when(jnp.logical_not(twin_first))
    def _():
        twin_terms()

    def rim_copy(side, who):
        return pltpu.make_async_remote_copy(
            src_ref=rim_sent.at[side], dst_ref=rim_got.at[side ^ 1],
            send_sem=rim_sem.at[0, side], recv_sem=rim_sem.at[1, side ^ 1],
            device_id=who, device_id_type=MESH,
        )

    def out_copy(kind, side):
        where = pl.ds(side * width, width)
        from_ref, to_ref = ((acc, sum_out), (rim_got, facing_out))[kind]
        return pltpu.make_async_copy(
            from_ref.at[side], to_ref.at[0, 0, :, where], out_sem.at[kind, side]
        )

    for side in range(4):
        there, who = neighbours[side]
        rim_sent[side] = (acc[side] * 0.25).astype(jnp.bfloat16)

        @pl.when(there)
        def _():
            rim_copy(side, who).start()

        @pl.when(jnp.logical_not(there))
        def _():
            rim_got[side] = jnp.zeros_like(rim_got[side])

        out_copy(0, side).start()

    load_classes.wait()
    total = jnp.zeros(coupling.shape, jnp.float32)
    for index in range(stiffness.shape[0]):
        total = total + jnp.where(classes[...] == index, stiffness[index], 0.0)
    coupling[...] = total
    coupling_copy = pltpu.make_async_copy(coupling, coupling_out.at[0], load_sem.at[2])
    coupling_copy.start()

    for side in range(4):
        there, who = neighbours[side]

        @pl.when(there)
        def _():
            rim_copy(side ^ 1, who).wait_recv()

        out_copy(1, side).start()

    for side in range(4):
        there, who = neighbours[side]

        @pl.when(there)
        def _():
            rim_copy(side, who).wait_send()

        out_copy(0, side).wait()
        out_copy(1, side).wait()
    coupling_copy.wait()
    all_shared(lambda copy: copy.wait_send())
    base_copy(0, 0).wait_send()
    for d in (0, 1):
        cross_copy(d).wait_send()

        @pl.when(gives_row)
        def _():
            for chunk in range(chunks):
                row_copy(d, chunk).wait_send()

        @pl.when(has_col(d))
        def _():
            relay_copy(d).wait_send()

        @pl.when(gives_col(d))
        def _():
            base_copy(1 + d, 0).wait_send()
            col_copy(d, 0).wait_send()
            col_copy(d, 1).wait_send()


def local(forcing, local_op, material, stiffness, *, row_count, col_count):
    _, _, loads, order = forcing.shape
    width = order // 4
    side = (loads, width)
    chunks = 2 if loads % 32 == 0 else 1
    any_spec = pl.BlockSpec(memory_space=pl.ANY)
    dma = pltpu.SemaphoreType.DMA
    f32, b16 = jnp.float32, jnp.bfloat16
    summed, facing, coupling = pl.pallas_call(
        functools.partial(kernel, row_count, col_count),
        out_shape=(
            jax.ShapeDtypeStruct(forcing.shape, f32),
            jax.ShapeDtypeStruct(forcing.shape, b16),
            jax.ShapeDtypeStruct(material.shape, f32),
        ),
        in_specs=[any_spec, any_spec, any_spec, pl.BlockSpec(memory_space=pltpu.SMEM)],
        out_specs=(any_spec,) * 3,
        scratch_shapes=[
            pltpu.VMEM((loads, order), f32),
            pltpu.VMEM((loads, order), b16),
            pltpu.VMEM((4, order, width), b16),
            pltpu.VMEM((4,) + side, f32),
            pltpu.VMEM((4,) + side, f32),
            pltpu.VMEM((2,) + side, f32),
            pltpu.VMEM(side, f32),
            pltpu.VMEM((7, width, width), b16),
            pltpu.VMEM((3,) + side, f32),
            pltpu.VMEM((width, width), b16),
            pltpu.VMEM((2,) + side, b16),
            pltpu.VMEM((2,) + side, b16),
            pltpu.VMEM((2,) + side, b16),
            pltpu.VMEM((2, 2) + side, b16),
            pltpu.VMEM((2, 2) + side, b16),
            pltpu.VMEM((2,) + side, b16),
            pltpu.VMEM((2,) + side, b16),
            pltpu.VMEM((4,) + side, b16),
            pltpu.VMEM((4,) + side, b16),
            pltpu.VMEM((1, order), f32),
            pltpu.VMEM((1, order), jnp.int32),
            dma((3,)),
            dma((4,)),
            dma((2, 4)),
            dma((2, 7)),
            dma((2, 3)),
            dma((2, 2, chunks)),
            dma((2, 2, 2)),
            dma((2, 2)),
            dma((2, 2)),
            dma((2, 4)),
        ],
        compiler_params=pltpu.CompilerParams(collective_id=0, has_side_effects=True),
    )(forcing, local_op, material, stiffness)
    preconditioned = summed * 0.25
    gap = facing.astype(f32) - preconditioned
    residual = forcing - preconditioned + coupling[:, :, None, :] * gap
    return preconditioned, residual


def solution(mesh):
    sizes = dict(mesh.shape)
    return jax.shard_map(
        functools.partial(local, row_count=sizes["row"], col_count=sizes["col"]),
        mesh=mesh,
        in_specs=(
            P("row", "col", None, None),
            P("row", "col", None, None),
            P("row", "col", None),
            P(),
        ),
        out_specs=(P("row", "col", None, None), P("row", "col", None, None)),
        check_vma=False,
    )
```

```python
import functools

import jax
import jax.numpy as jnp
from jax import lax
from jax.experimental import pallas as pl
from jax.experimental.pallas import tpu as pltpu
from jax.sharding import PartitionSpec as P

MESH = pl.DeviceIdType.MESH


def kernel(
    row_count, col_count, forcing, op, material, stiffness, sum_out, facing_out, coupling_out,
    source, half, mat, base, acc, tmp_row, tmp_col, twin_mat, twin_base, hop, cross,
    row_sent, row_got, col_sent, col_got, twin_row, twin_col, rim_sent, rim_got, coupling, classes,
    load_sem, op_sem, out_sem, mat_sem, base_sem, row_sem, col_sem, cross_sem, relay_sem, rim_sem,
):
    width = base.shape[-1]
    chunks = row_sem.shape[-1]
    span = base.shape[1] // chunks
    row = lax.axis_index("row")
    col = lax.axis_index("col")
    core = row % 2
    pair = row // 2
    pair_count = row_count // 2
    step = 1 - 2 * core
    twin = row + step
    in_row, out_row = core, 1 - core
    left, right = col > 0, col < col_count - 1
    has_row = jnp.where(core == 0, pair, pair_count - 1 - pair) > 0
    gives_row = jnp.where(core == 0, pair_count - 1 - pair, pair) > 0

    def columns(side):
        return pl.ds(pl.multiple_of(side * width, width), width)

    def remote(src, dst, sem, place, who):
        return pltpu.make_async_remote_copy(
            src_ref=src, dst_ref=dst, send_sem=sem.at[(0,) + place], recv_sem=sem.at[(1,) + place],
            device_id=who, device_id_type=MESH,
        )

    def dot(left_value, right_value):
        return jnp.dot(left_value, right_value, preferred_element_type=jnp.float32)

    first = jnp.where(col <= col_count - 1 - col, 0, 1)
    low_half = pair * 2 < pair_count
    order = [jnp.where(low_half, 1, 0), 3 - first, 2 + first, jnp.where(low_half, 0, 1)]
    load_forcing = pltpu.make_async_copy(forcing.at[0, 0], source, load_sem.at[0])
    load_classes = pltpu.make_async_copy(material.at[0], classes, load_sem.at[1])

    def load_op(side):
        return pltpu.make_async_copy(op.at[0, 0, :, columns(side)], mat.at[side], op_sem.at[side])

    load_forcing.start()
    load_op(order[0]).start()

    partners = (
        (row > 0, {"row": row - 1}), (row < row_count - 1, {"row": row + 1}),
        (row > 1, {"row": row - 2}), (row < row_count - 2, {"row": row + 2}),
        (left, {"col": col - 1}), (right, {"col": col + 1}),
    )
    neighbours = (partners[0], partners[1], partners[4], partners[5])
    barrier = pltpu.get_barrier_semaphore()
    for there, who in partners:
        @pl.when(there)
        def _(who=who):
            pl.semaphore_signal(barrier, inc=1, device_id=who, device_id_type=MESH)
    pl.semaphore_wait(barrier, sum(jnp.where(there, 1, 0) for there, _ in partners))

    def has_col(d):
        return jnp.where(d == 0, col, col_count - 1 - col) > 0

    def gives_col(d):
        return jnp.where(d == 0, col_count - 1 - col, col) > 0

    def mat_copy(slot, in_side, out_side):
        return remote(
            op.at[0, 0, columns(in_side), columns(out_side)], twin_mat.at[slot], mat_sem, (slot,),
            {"row": twin},
        )

    twin_in, twin_out = 1 - core, core
    shared = []
    for d in (0, 1):
        enters, leaves = has_col(d), gives_col(d)
        shared.append((leaves, 1 + 3 * d, twin_in, 3 - d))
        shared.append((enters, 2 + 3 * d, 2 + d, twin_out))
        shared.append((jnp.logical_and(enters, leaves), 3 + 3 * d, 2 + d, 3 - d))

    def all_shared(act):
        for there, slot, in_side, out_side in shared:
            @pl.when(there)
            def _(slot=slot, in_side=in_side, out_side=out_side):
                act(mat_copy(slot, in_side, out_side))

    mat_copy(0, twin_in, twin_out).start()

    def base_copy(slot, side):
        return remote(base.at[side], twin_base.at[slot], base_sem, (slot,), {"row": twin})

    load_forcing.wait()
    half[...] = source[...].astype(jnp.bfloat16)

    def make_base(side, after=lambda: None):
        load_op(side).wait()
        after()
        base[side] = dot(half[...], mat[side])

        @pl.when(side == twin_out)
        def _():
            base_copy(0, side).start()

        for d in (0, 1):
            @pl.when(jnp.logical_and(side == 3 - d, gives_col(d)))
            def _(d=d):
                base_copy(1 + d, side).start()

    def row_copy(d, chunk):
        part = pl.ds(chunk * span, span)
        return remote(
            row_sent.at[d, part], row_got.at[d, part], row_sem, (d, chunk), {"row": row + 2 * step}
        )

    def col_copy(d, cell):
        return remote(
            col_sent.at[d, cell], col_got.at[d, cell], col_sem, (d, cell), {"col": col + 1 - 2 * d}
        )

    def cross_copy(d):
        return remote(cross.at[d], twin_row.at[d], cross_sem, (d,), {"row": twin})

    def relay_copy(d):
        return remote(col_got.at[d, 1], twin_col.at[d], relay_sem, (d,), {"row": twin})

    def wait_shared():
        base_copy(0, 0).wait_recv()
        mat_copy(0, 0, 0).wait_recv()

    def solve_row(d):
        in_col = 2 + d
        enters = has_col(d)
        tmp_row[0] = base[out_row]
        tmp_row[1] = twin_base[0]

        @pl.when(enters)
        def _():
            col_copy(d, 0).wait_recv()
            tmp_row[0] += dot(col_got[d, 0], mat[out_row, columns(in_col), :])

        @pl.when(gives_row)
        def _():
            tmp_row[1] += dot(tmp_row[0].astype(jnp.bfloat16), twin_mat[0])

        @pl.when(enters)
        def _():
            mat_copy(2 + 3 * d, 0, 0).wait_recv()
            col_copy(d, 1).wait_recv()
            relay_copy(d).start()
            tmp_row[1] += dot(col_got[d, 1], twin_mat[2 + 3 * d])

        for chunk in range(chunks):
            part = pl.ds(chunk * span, span)

            @pl.when(has_row)
            def _():
                row_copy(d, chunk).wait_recv()

            @pl.when(jnp.logical_and(has_row, gives_row))
            def _():
                row_sent[d, part] = (
                    tmp_row[1, part] + dot(row_got[d, part], hop[...])
                ).astype(jnp.bfloat16)
                row_copy(d, chunk).start()

            @pl.when(jnp.logical_and(jnp.logical_not(has_row), gives_row))
            def _():
                row_sent[d, part] = tmp_row[1, part].astype(jnp.bfloat16)
                row_copy(d, chunk).start()

        @pl.when(has_row)
        def _():
            tmp_row[0] += dot(row_got[d], mat[out_row, columns(in_row), :])

        cross[d] = tmp_row[0].astype(jnp.bfloat16)
        cross_copy(d).start()

    def solve_col(d):
        in_col, out_col = 2 + d, 3 - d
        enters, leaves = has_col(d), gives_col(d)

        @pl.when(leaves)
        def _():
            tmp_col[...] = base[out_col]

            @pl.when(enters)
            def _():
                tmp_col[...] += dot(col_got[d, 0], mat[out_col, columns(in_col), :])

            @pl.when(has_row)
            def _():
                tmp_col[...] += dot(row_got[d], mat[out_col, columns(in_row), :])

            col_sent[d, 0] = tmp_col[...].astype(jnp.bfloat16)
            col_copy(d, 0).start()
            base_copy(1 + d, 0).wait_recv()
            mat_copy(1 + 3 * d, 0, 0).wait_recv()
            tmp_col[...] = twin_base[1 + d] + dot(cross[d], twin_mat[1 + 3 * d])

            @pl.when(enters)
            def _():
                mat_copy(3 + 3 * d, 0, 0).wait_recv()
                tmp_col[...] += dot(col_got[d, 1], twin_mat[3 + 3 * d])

            col_sent[d, 1] = tmp_col[...].astype(jnp.bfloat16)
            col_copy(d, 1).start()

    def add_terms(trace, in_side):
        for side in range(4):
            acc[side] += dot(trace[...], mat[side, columns(in_side), :])

    def own_terms(d):
        @pl.when(has_row)
        def _():
            add_terms(row_got.at[d], in_row)

        @pl.when(has_col(d))
        def _():
            add_terms(col_got.at[d, 0], 2 + d)

    def twin_terms():
        def one(position, carry):
            d = jnp.where(position == 0, first, 1 - first)

            @pl.when(has_col(d))
            def _():
                relay_copy(d).wait_recv()
                add_terms(twin_col.at[d], 2 + d)

            cross_copy(d).wait_recv()
            add_terms(twin_row.at[d], 1 - core)
            return carry

        lax.fori_loop(0, 2, one, 0)

    early = jnp.logical_and(
        jnp.where(low_half, 0, 1) == core,
        jnp.logical_not(jnp.logical_or(has_row, has_col(first))),
    )

    def other_loads():
        for side in order[1:]:
            load_op(side).start()
        load_classes.start()
        all_shared(lambda copy: copy.start())

    make_base(order[0], other_loads)

    @pl.when(early)
    def _():
        wait_shared()
        solve_row(first)

    make_base(order[1])

    @pl.when(early)
    def _():
        solve_col(first)

    make_base(order[2])
    make_base(order[3])
    acc[...] = base[...] * 4.0

    @pl.when(jnp.logical_not(early))
    def _():
        wait_shared()

    @pl.when(jnp.logical_and(has_row, gives_row))
    def _():
        hop[...] = dot(mat[out_row, columns(in_row), :], twin_mat[0]).astype(jnp.bfloat16)

    depth = jnp.where(core == 0, pair, pair_count - 1 - pair)
    twin_first = depth * 2 >= pair_count + 2

    @pl.when(twin_first)
    def _():
        twin_terms()

    @pl.when(jnp.logical_not(early))
    def _():
        solve_row(first)
        solve_col(first)

    own_terms(first)
    solve_row(1 - first)
    solve_col(1 - first)
    own_terms(1 - first)

    @pl.when(jnp.logical_not(twin_first))
    def _():
        twin_terms()

    def rim_copy(side, who):
        return pltpu.make_async_remote_copy(
            src_ref=rim_sent.at[side], dst_ref=rim_got.at[side ^ 1],
            send_sem=rim_sem.at[0, side], recv_sem=rim_sem.at[1, side ^ 1],
            device_id=who, device_id_type=MESH,
        )

    def out_copy(kind, side):
        where = pl.ds(side * width, width)
        from_ref, to_ref = ((acc, sum_out), (rim_got, facing_out))[kind]
        return pltpu.make_async_copy(
            from_ref.at[side], to_ref.at[0, 0, :, where], out_sem.at[kind, side]
        )

    for side in (2, 3, 0, 1):
        there, who = neighbours[side]
        rim_sent[side] = (acc[side] * 0.25).astype(jnp.bfloat16)

        @pl.when(there)
        def _():
            rim_copy(side, who).start()

        @pl.when(jnp.logical_not(there))
        def _():
            rim_got[side] = jnp.zeros_like(rim_got[side])

        out_copy(0, side).start()

    load_classes.wait()
    total = jnp.zeros(coupling.shape, jnp.float32)
    for index in range(stiffness.shape[0]):
        total = total + jnp.where(classes[...] == index, stiffness[index], 0.0)
    coupling[...] = total
    coupling_copy = pltpu.make_async_copy(coupling, coupling_out.at[0], load_sem.at[2])
    coupling_copy.start()

    for side in range(4):
        there, who = neighbours[side]

        @pl.when(there)
        def _():
            rim_copy(side ^ 1, who).wait_recv()

        out_copy(1, side).start()

    for side in range(4):
        there, who = neighbours[side]

        @pl.when(there)
        def _():
            rim_copy(side, who).wait_send()

        out_copy(0, side).wait()
        out_copy(1, side).wait()
    coupling_copy.wait()
    mat_copy(0, 0, 0).wait_send()
    all_shared(lambda copy: copy.wait_send())
    base_copy(0, 0).wait_send()
    for d in (0, 1):
        cross_copy(d).wait_send()

        @pl.when(gives_row)
        def _():
            for chunk in range(chunks):
                row_copy(d, chunk).wait_send()

        @pl.when(has_col(d))
        def _():
            relay_copy(d).wait_send()

        @pl.when(gives_col(d))
        def _():
            base_copy(1 + d, 0).wait_send()
            col_copy(d, 0).wait_send()
            col_copy(d, 1).wait_send()


def local(forcing, local_op, material, stiffness, *, row_count, col_count):
    _, _, loads, order = forcing.shape
    width = order // 4
    side = (loads, width)
    chunks = 2 if loads % 32 == 0 else 1
    any_spec = pl.BlockSpec(memory_space=pl.ANY)
    dma = pltpu.SemaphoreType.DMA
    f32, b16 = jnp.float32, jnp.bfloat16
    summed, facing, coupling = pl.pallas_call(
        functools.partial(kernel, row_count, col_count),
        out_shape=(
            jax.ShapeDtypeStruct(forcing.shape, f32),
            jax.ShapeDtypeStruct(forcing.shape, b16),
            jax.ShapeDtypeStruct(material.shape, f32),
        ),
        in_specs=[any_spec, any_spec, any_spec, pl.BlockSpec(memory_space=pltpu.SMEM)],
        out_specs=(any_spec,) * 3,
        scratch_shapes=[
            pltpu.VMEM((loads, order), f32),
            pltpu.VMEM((loads, order), b16),
            pltpu.VMEM((4, order, width), b16),
            pltpu.VMEM((4,) + side, f32),
            pltpu.VMEM((4,) + side, f32),
            pltpu.VMEM((2,) + side, f32),
            pltpu.VMEM(side, f32),
            pltpu.VMEM((7, width, width), b16),
            pltpu.VMEM((3,) + side, f32),
            pltpu.VMEM((width, width), b16),
            pltpu.VMEM((2,) + side, b16),
            pltpu.VMEM((2,) + side, b16),
            pltpu.VMEM((2,) + side, b16),
            pltpu.VMEM((2, 2) + side, b16),
            pltpu.VMEM((2, 2) + side, b16),
            pltpu.VMEM((2,) + side, b16),
            pltpu.VMEM((2,) + side, b16),
            pltpu.VMEM((4,) + side, b16),
            pltpu.VMEM((4,) + side, b16),
            pltpu.VMEM((1, order), f32),
            pltpu.VMEM((1, order), jnp.int32),
            dma((3,)),
            dma((4,)),
            dma((2, 4)),
            dma((2, 7)),
            dma((2, 3)),
            dma((2, 2, chunks)),
            dma((2, 2, 2)),
            dma((2, 2)),
            dma((2, 2)),
            dma((2, 4)),
        ],
        compiler_params=pltpu.CompilerParams(collective_id=0, has_side_effects=True),
    )(forcing, local_op, material, stiffness)
    preconditioned = summed * 0.25
    gap = facing.astype(f32) - preconditioned
    residual = forcing - preconditioned + coupling[:, :, None, :] * gap
    return preconditioned, residual


def solution(mesh):
    sizes = dict(mesh.shape)
    return jax.shard_map(
        functools.partial(local, row_count=sizes["row"], col_count=sizes["col"]),
        mesh=mesh,
        in_specs=(
            P("row", "col", None, None),
            P("row", "col", None, None),
            P("row", "col", None),
            P(),
        ),
        out_specs=(P("row", "col", None, None), P("row", "col", None, None)),
        check_vma=False,
    )
```

```python
import functools

import jax
import jax.numpy as jnp
from jax import lax
from jax.experimental import pallas as pl
from jax.experimental.pallas import tpu as pltpu
from jax.sharding import PartitionSpec as P

MESH = pl.DeviceIdType.MESH


def kernel(
    row_count, col_count, forcing, op, material, stiffness, sum_out, facing_out, coupling_out,
    source, half, mat, base, acc, tmp_row, tmp_col, twin_mat, twin_base, hop, cross,
    row_sent, row_got, col_sent, col_got, twin_row, twin_col, rim_sent, rim_got, coupling, classes,
    load_sem, op_sem, out_sem, mat_sem, base_sem, row_sem, col_sem, cross_sem, relay_sem, rim_sem,
):
    width = base.shape[-1]
    chunks = row_sem.shape[-1]
    span = base.shape[1] // chunks
    row = lax.axis_index("row")
    col = lax.axis_index("col")
    core = row % 2
    pair = row // 2
    pair_count = row_count // 2
    step = 1 - 2 * core
    twin = row + step
    in_row, out_row = core, 1 - core
    left, right = col > 0, col < col_count - 1
    has_row = jnp.where(core == 0, pair, pair_count - 1 - pair) > 0
    gives_row = jnp.where(core == 0, pair_count - 1 - pair, pair) > 0

    def columns(side):
        return pl.ds(pl.multiple_of(side * width, width), width)

    def remote(src, dst, sem, place, who):
        return pltpu.make_async_remote_copy(
            src_ref=src, dst_ref=dst, send_sem=sem.at[(0,) + place], recv_sem=sem.at[(1,) + place],
            device_id=who, device_id_type=MESH,
        )

    def dot(left_value, right_value):
        return jnp.dot(left_value, right_value, preferred_element_type=jnp.float32)

    first = jnp.where(col <= col_count - 1 - col, 0, 1)
    low_half = pair * 2 < pair_count
    order = [jnp.where(low_half, 1, 0), 3 - first, 2 + first, jnp.where(low_half, 0, 1)]
    load_forcing = pltpu.make_async_copy(forcing.at[0, 0], source, load_sem.at[0])
    load_classes = pltpu.make_async_copy(material.at[0], classes, load_sem.at[1])

    def load_op(side):
        return pltpu.make_async_copy(op.at[0, 0, :, columns(side)], mat.at[side], op_sem.at[side])

    load_forcing.start()
    load_op(order[0]).start()

    partners = (
        (row > 0, {"row": row - 1}), (row < row_count - 1, {"row": row + 1}),
        (row > 1, {"row": row - 2}), (row < row_count - 2, {"row": row + 2}),
        (left, {"col": col - 1}), (right, {"col": col + 1}),
    )
    neighbours = (partners[0], partners[1], partners[4], partners[5])
    barrier = pltpu.get_barrier_semaphore()
    for there, who in partners:
        @pl.when(there)
        def _(who=who):
            pl.semaphore_signal(barrier, inc=1, device_id=who, device_id_type=MESH)
    pl.semaphore_wait(barrier, sum(jnp.where(there, 1, 0) for there, _ in partners))

    def has_col(d):
        return jnp.where(d == 0, col, col_count - 1 - col) > 0

    def gives_col(d):
        return jnp.where(d == 0, col_count - 1 - col, col) > 0

    def mat_copy(slot, in_side, out_side):
        return remote(
            op.at[0, 0, columns(in_side), columns(out_side)], twin_mat.at[slot], mat_sem, (slot,),
            {"row": twin},
        )

    twin_in, twin_out = 1 - core, core
    shared = []
    for d in (0, 1):
        enters, leaves = has_col(d), gives_col(d)
        shared.append((leaves, 1 + 3 * d, twin_in, 3 - d))
        shared.append((enters, 2 + 3 * d, 2 + d, twin_out))
        shared.append((jnp.logical_and(enters, leaves), 3 + 3 * d, 2 + d, 3 - d))

    def all_shared(act):
        for there, slot, in_side, out_side in shared:
            @pl.when(there)
            def _(slot=slot, in_side=in_side, out_side=out_side):
                act(mat_copy(slot, in_side, out_side))

    mat_copy(0, twin_in, twin_out).start()

    def base_copy(slot, side):
        return remote(base.at[side], twin_base.at[slot], base_sem, (slot,), {"row": twin})

    load_forcing.wait()
    half[...] = source[...].astype(jnp.bfloat16)

    def make_base(side, after=lambda: None):
        load_op(side).wait()
        after()
        base[side] = dot(half[...], mat[side])

        @pl.when(side == twin_out)
        def _():
            base_copy(0, side).start()

        for d in (0, 1):
            @pl.when(jnp.logical_and(side == 3 - d, gives_col(d)))
            def _(d=d):
                base_copy(1 + d, side).start()

    def row_copy(d, chunk):
        part = pl.ds(chunk * span, span)
        return remote(
            row_sent.at[d, part], row_got.at[d, part], row_sem, (d, chunk), {"row": row + 2 * step}
        )

    def col_copy(d, cell):
        return remote(
            col_sent.at[d, cell], col_got.at[d, cell], col_sem, (d, cell), {"col": col + 1 - 2 * d}
        )

    def cross_copy(d):
        return remote(cross.at[d], twin_row.at[d], cross_sem, (d,), {"row": twin})

    def relay_copy(d):
        return remote(col_got.at[d, 1], twin_col.at[d], relay_sem, (d,), {"row": twin})

    def wait_shared():
        base_copy(0, 0).wait_recv()
        mat_copy(0, 0, 0).wait_recv()

    def solve_row(d):
        in_col = 2 + d
        enters = has_col(d)
        tmp_row[0] = base[out_row]
        tmp_row[1] = twin_base[0]

        @pl.when(enters)
        def _():
            col_copy(d, 0).wait_recv()
            tmp_row[0] += dot(col_got[d, 0], mat[out_row, columns(in_col), :])

        @pl.when(gives_row)
        def _():
            tmp_row[1] += dot(tmp_row[0].astype(jnp.bfloat16), twin_mat[0])

        @pl.when(enters)
        def _():
            mat_copy(2 + 3 * d, 0, 0).wait_recv()
            col_copy(d, 1).wait_recv()
            relay_copy(d).start()
            tmp_row[1] += dot(col_got[d, 1], twin_mat[2 + 3 * d])

        for chunk in range(chunks):
            part = pl.ds(chunk * span, span)

            @pl.when(has_row)
            def _():
                row_copy(d, chunk).wait_recv()

            @pl.when(jnp.logical_and(has_row, gives_row))
            def _():
                row_sent[d, part] = (
                    tmp_row[1, part] + dot(row_got[d, part], hop[...])
                ).astype(jnp.bfloat16)
                row_copy(d, chunk).start()

            @pl.when(jnp.logical_and(jnp.logical_not(has_row), gives_row))
            def _():
                row_sent[d, part] = tmp_row[1, part].astype(jnp.bfloat16)
                row_copy(d, chunk).start()

        @pl.when(has_row)
        def _():
            tmp_row[0] += dot(row_got[d], mat[out_row, columns(in_row), :])

        cross[d] = tmp_row[0].astype(jnp.bfloat16)
        cross_copy(d).start()

    def solve_col(d):
        in_col, out_col = 2 + d, 3 - d
        enters, leaves = has_col(d), gives_col(d)

        @pl.when(leaves)
        def _():
            tmp_col[...] = base[out_col]

            @pl.when(enters)
            def _():
                tmp_col[...] += dot(col_got[d, 0], mat[out_col, columns(in_col), :])

            @pl.when(has_row)
            def _():
                tmp_col[...] += dot(row_got[d], mat[out_col, columns(in_row), :])

            col_sent[d, 0] = tmp_col[...].astype(jnp.bfloat16)
            col_copy(d, 0).start()
            base_copy(1 + d, 0).wait_recv()
            mat_copy(1 + 3 * d, 0, 0).wait_recv()
            tmp_col[...] = twin_base[1 + d] + dot(cross[d], twin_mat[1 + 3 * d])

            @pl.when(enters)
            def _():
                mat_copy(3 + 3 * d, 0, 0).wait_recv()
                tmp_col[...] += dot(col_got[d, 1], twin_mat[3 + 3 * d])

            col_sent[d, 1] = tmp_col[...].astype(jnp.bfloat16)
            col_copy(d, 1).start()

    def add_terms(trace, in_side):
        for side in range(4):
            acc[side] += dot(trace[...], mat[side, columns(in_side), :])

    def own_terms(d):
        @pl.when(has_row)
        def _():
            add_terms(row_got.at[d], in_row)

        @pl.when(has_col(d))
        def _():
            add_terms(col_got.at[d, 0], 2 + d)

    def twin_terms():
        def one(position, carry):
            d = jnp.where(position == 0, first, 1 - first)

            @pl.when(has_col(d))
            def _():
                relay_copy(d).wait_recv()
                add_terms(twin_col.at[d], 2 + d)

            cross_copy(d).wait_recv()
            add_terms(twin_row.at[d], 1 - core)
            return carry

        lax.fori_loop(0, 2, one, 0)

    early = jnp.logical_and(
        jnp.where(low_half, 0, 1) == core,
        jnp.logical_not(jnp.logical_or(has_row, has_col(first))),
    )

    def other_loads():
        for side in order[1:]:
            load_op(side).start()
        load_classes.start()
        all_shared(lambda copy: copy.start())

    make_base(order[0], other_loads)

    @pl.when(early)
    def _():
        wait_shared()
        solve_row(first)

    make_base(order[1])

    @pl.when(early)
    def _():
        solve_col(first)

    make_base(order[2])
    make_base(order[3])
    acc[...] = base[...] * 4.0

    @pl.when(jnp.logical_not(early))
    def _():
        wait_shared()

    @pl.when(jnp.logical_and(has_row, gives_row))
    def _():
        hop[...] = dot(mat[out_row, columns(in_row), :], twin_mat[0]).astype(jnp.bfloat16)

    depth = jnp.where(core == 0, pair, pair_count - 1 - pair)
    twin_first = depth * 2 >= pair_count + 2

    @pl.when(twin_first)
    def _():
        twin_terms()

    @pl.when(jnp.logical_not(early))
    def _():
        solve_row(first)
        solve_col(first)

    own_terms(first)
    solve_row(1 - first)
    solve_col(1 - first)
    own_terms(1 - first)

    @pl.when(jnp.logical_not(twin_first))
    def _():
        twin_terms()

    def rim_copy(side, who):
        return pltpu.make_async_remote_copy(
            src_ref=rim_sent.at[side], dst_ref=rim_got.at[side ^ 1],
            send_sem=rim_sem.at[0, side], recv_sem=rim_sem.at[1, side ^ 1],
            device_id=who, device_id_type=MESH,
        )

    def out_copy(kind, side):
        where = pl.ds(side * width, width)
        from_ref, to_ref = ((acc, sum_out), (rim_got, facing_out))[kind]
        return pltpu.make_async_copy(
            from_ref.at[side], to_ref.at[0, 0, :, where], out_sem.at[kind, side]
        )

    for side in (2, 3, 0, 1):
        there, who = neighbours[side]
        rim_sent[side] = (acc[side] * 0.25).astype(jnp.bfloat16)

        @pl.when(there)
        def _():
            rim_copy(side, who).start()

        @pl.when(jnp.logical_not(there))
        def _():
            rim_got[side] = jnp.zeros_like(rim_got[side])

        out_copy(0, side).start()

    load_classes.wait()
    total = jnp.zeros(coupling.shape, jnp.float32)
    for index in range(stiffness.shape[0]):
        total = total + jnp.where(classes[...] == index, stiffness[index], 0.0)
    coupling[...] = total
    coupling_copy = pltpu.make_async_copy(coupling, coupling_out.at[0], load_sem.at[2])
    coupling_copy.start()

    for side in range(4):
        there, who = neighbours[side]

        @pl.when(there)
        def _():
            rim_copy(side ^ 1, who).wait_recv()

        out_copy(1, side).start()

    for side in range(4):
        there, who = neighbours[side]

        @pl.when(there)
        def _():
            rim_copy(side, who).wait_send()

        out_copy(0, side).wait()
        out_copy(1, side).wait()
    coupling_copy.wait()
    mat_copy(0, 0, 0).wait_send()
    all_shared(lambda copy: copy.wait_send())
    base_copy(0, 0).wait_send()
    for d in (0, 1):
        cross_copy(d).wait_send()

        @pl.when(gives_row)
        def _():
            for chunk in range(chunks):
                row_copy(d, chunk).wait_send()

        @pl.when(has_col(d))
        def _():
            relay_copy(d).wait_send()

        @pl.when(gives_col(d))
        def _():
            base_copy(1 + d, 0).wait_send()
            col_copy(d, 0).wait_send()
            col_copy(d, 1).wait_send()


def local(forcing, local_op, material, stiffness, *, row_count, col_count):
    _, _, loads, order = forcing.shape
    width = order // 4
    side = (loads, width)
    chunks = next(n for n in (3, 2, 1) if loads % (16 * n) == 0)
    any_spec = pl.BlockSpec(memory_space=pl.ANY)
    dma = pltpu.SemaphoreType.DMA
    f32, b16 = jnp.float32, jnp.bfloat16
    summed, facing, coupling = pl.pallas_call(
        functools.partial(kernel, row_count, col_count),
        out_shape=(
            jax.ShapeDtypeStruct(forcing.shape, f32),
            jax.ShapeDtypeStruct(forcing.shape, b16),
            jax.ShapeDtypeStruct(material.shape, f32),
        ),
        in_specs=[any_spec, any_spec, any_spec, pl.BlockSpec(memory_space=pltpu.SMEM)],
        out_specs=(any_spec,) * 3,
        scratch_shapes=[
            pltpu.VMEM((loads, order), f32),
            pltpu.VMEM((loads, order), b16),
            pltpu.VMEM((4, order, width), b16),
            pltpu.VMEM((4,) + side, f32),
            pltpu.VMEM((4,) + side, f32),
            pltpu.VMEM((2,) + side, f32),
            pltpu.VMEM(side, f32),
            pltpu.VMEM((7, width, width), b16),
            pltpu.VMEM((3,) + side, f32),
            pltpu.VMEM((width, width), b16),
            pltpu.VMEM((2,) + side, b16),
            pltpu.VMEM((2,) + side, b16),
            pltpu.VMEM((2,) + side, b16),
            pltpu.VMEM((2, 2) + side, b16),
            pltpu.VMEM((2, 2) + side, b16),
            pltpu.VMEM((2,) + side, b16),
            pltpu.VMEM((2,) + side, b16),
            pltpu.VMEM((4,) + side, b16),
            pltpu.VMEM((4,) + side, b16),
            pltpu.VMEM((1, order), f32),
            pltpu.VMEM((1, order), jnp.int32),
            dma((3,)),
            dma((4,)),
            dma((2, 4)),
            dma((2, 7)),
            dma((2, 3)),
            dma((2, 2, chunks)),
            dma((2, 2, 2)),
            dma((2, 2)),
            dma((2, 2)),
            dma((2, 4)),
        ],
        compiler_params=pltpu.CompilerParams(collective_id=0, has_side_effects=True),
    )(forcing, local_op, material, stiffness)
    preconditioned = summed * 0.25
    gap = facing.astype(f32) - preconditioned
    residual = forcing - preconditioned + coupling[:, :, None, :] * gap
    return preconditioned, residual


def solution(mesh):
    sizes = dict(mesh.shape)
    return jax.shard_map(
        functools.partial(local, row_count=sizes["row"], col_count=sizes["col"]),
        mesh=mesh,
        in_specs=(
            P("row", "col", None, None),
            P("row", "col", None, None),
            P("row", "col", None),
            P(),
        ),
        out_specs=(P("row", "col", None, None), P("row", "col", None, None)),
        check_vma=False,
    )
```
